32 devices in a mesh: rows: 4 (over y, x), cols: 8 (over z, core).
Axes of the slice: x: 2, y: 2, z: 4, core: 2. Of those that a mesh axis runs over, the one named last changes fastest.
Arguments:
- anomalies: float32 [16384, 1024], P('rows', 'cols'), may hold values from -75 to 75
- pairing: int32 [2, 8], replicated, may hold values from 0 to 7, as said below
Outputs:
- rotated: float32 [16384, 1024], P('rows', 'cols')
The draws below stay inside these ranges and needn't reach their ends.
Inputs may be any that keep to these rules, and one draw needn't show every extreme that they name: pairing[r, b] = b XOR m_r with one m_r for the whole row r; m_0 is neither 0 nor 1024 // 128 - 1, and for odd r m_r is m_0 with every bit of 7 flipped, for even r it is m_0.
All inputs are finite; a program needn't handle non-finite values.
Results may differ from the reference program's by a relative error of at most 0.0003.
Values sent between devices are 32-bit elements; how exact they have to be, the bound alone decides.
A program may use at most 128 MiB of HBM per device.

```python
import math
import jax
import jax.numpy as jnp
from jax import lax

BLK = 128
SHIFTS = 8
ROUNDS = 2
SOUNDINGS = 16384
MEMBERS = 1024


def draw_anomalies(key, part):
    subkeys = jax.random.split(key, 5)
    position = (jnp.arange(SOUNDINGS, dtype=jnp.float32)[:, None] + 0.5) / SOUNDINGS
    rising = 1.0 + 2.0 * position
    roughness = jax.random.uniform(subkeys[0], (SOUNDINGS, 1), jnp.float32, 0.5, 1.5)
    column_scale = jnp.exp(jax.random.uniform(subkeys[1], (1, MEMBERS), jnp.float32, math.log(0.3), math.log(3.0)))
    row_factor = jnp.clip(jax.random.normal(subkeys[2], (SOUNDINGS, 1), jnp.float32), -5.0, 5.0)
    column_factor = jnp.clip(jax.random.normal(subkeys[3], (1, MEMBERS), jnp.float32), -5.0, 5.0)
    noise_field = jnp.clip(jax.random.normal(subkeys[4], (SOUNDINGS, MEMBERS), jnp.float32), -5.0, 5.0)
    strength = 0.2 + 0.8 * position
    values = 0.3 * rising * roughness * (noise_field * column_scale + strength * row_factor * column_factor)
    return values.astype(jnp.float32)


def draw_pairing(key, part):
    block_total = MEMBERS // BLK
    first_mask = jax.random.randint(key, (), 1, block_total - 1)
    all_bits = block_total - 1
    round_ids = jnp.arange(ROUNDS)
    round_masks = jnp.where(round_ids % 2 == 0, first_mask, jnp.bitwise_xor(first_mask, all_bits))
    indices = jnp.arange(block_total)
    return jnp.bitwise_xor(indices[None, :], round_masks[:, None]).astype(jnp.int32)


def setup_inputs(seed: int = 0) -> dict:
    arg_keys = jax.random.split(jax.random.key(seed), 3)
    return {
        "anomalies": draw_anomalies(jax.random.fold_in(arg_keys[2], 71), 0),
        "pairing": draw_pairing(jax.random.fold_in(arg_keys[2], 71), 0),
    }


TIE_GUARD = 1e-06

def block_product(left, right):
    return jnp.dot(left.T, right, precision=lax.Precision.HIGHEST, preferred_element_type=jnp.float32)

def apply_turn(data, coef):
    return jnp.dot(data, coef, precision=lax.Precision.HIGHEST, preferred_element_type=jnp.float32)

def rotate_pair(gram_ll, gram_lr, gram_rl, gram_rr, shifts):
    width = gram_ll.shape[0]
    eye_block = jnp.eye(width, dtype=jnp.float32)
    empty_block = jnp.zeros((width, width), jnp.float32)
    turn_ll, turn_lr, turn_rl, turn_rr = (eye_block, empty_block, empty_block, eye_block)
    for shift_step in range(shifts):
        if shift_step > 0:
            gram_lr = jnp.roll(gram_lr, -1, axis=1)
            gram_rl = jnp.roll(gram_rl, -1, axis=0)
            gram_rr = jnp.roll(jnp.roll(gram_rr, -1, axis=0), -1, axis=1)
            turn_lr = jnp.roll(turn_lr, -1, axis=1)
            turn_rr = jnp.roll(turn_rr, -1, axis=1)
        left_diag = jnp.diagonal(gram_ll)
        right_diag = jnp.diagonal(gram_rr)
        cross_diag = jnp.diagonal(gram_lr)
        gap_value = right_diag - left_diag
        gap_sign = jnp.where(gap_value >= 0.0, 1.0, -1.0).astype(gap_value.dtype)
        denom = jnp.abs(gap_value) + jnp.sqrt(gap_value * gap_value + 4.0 * cross_diag * cross_diag) + TIE_GUARD * (left_diag + right_diag)
        tangent = 2.0 * cross_diag * gap_sign / denom
        cosine = 1.0 / jnp.sqrt(1.0 + tangent * tangent)
        sine_value = cosine * tangent
        col_cos = cosine[None, :]
        col_sin = sine_value[None, :]
        upper_left = gram_ll * col_cos - gram_lr * col_sin
        upper_right = gram_ll * col_sin + gram_lr * col_cos
        lower_left = gram_rl * col_cos - gram_rr * col_sin
        lower_right = gram_rl * col_sin + gram_rr * col_cos
        row_cos = cosine[:, None]
        row_sin = sine_value[:, None]
        gram_ll = row_cos * upper_left - row_sin * lower_left
        gram_lr = row_cos * upper_right - row_sin * lower_right
        gram_rl = row_sin * upper_left + row_cos * lower_left
        gram_rr = row_sin * upper_right + row_cos * lower_right
        new_ll = turn_ll * col_cos - turn_lr * col_sin
        new_lr = turn_ll * col_sin + turn_lr * col_cos
        new_rl = turn_rl * col_cos - turn_rr * col_sin
        new_rr = turn_rl * col_sin + turn_rr * col_cos
        turn_ll, turn_lr, turn_rl, turn_rr = (new_ll, new_lr, new_rl, new_rr)
    back_steps = shifts - 1
    turn_lr = jnp.roll(turn_lr, back_steps, axis=1)
    turn_rr = jnp.roll(turn_rr, back_steps, axis=1)
    gram_rr = jnp.roll(jnp.roll(gram_rr, back_steps, axis=0), back_steps, axis=1)
    return ((turn_ll, turn_lr, turn_rl, turn_rr), (gram_ll, gram_rr))

def pair_output(current, pair_row, block_index):
    partner = pair_row[block_index].astype(jnp.int32)
    low_index = jnp.minimum(block_index, partner).astype(jnp.int32)
    high_index = jnp.maximum(block_index, partner).astype(jnp.int32)
    low_cols = lax.dynamic_slice_in_dim(current, (low_index * BLK).astype(jnp.int32), BLK, 1)
    high_cols = lax.dynamic_slice_in_dim(current, (high_index * BLK).astype(jnp.int32), BLK, 1)
    gram_ll = block_product(low_cols, low_cols)
    gram_lr = block_product(low_cols, high_cols)
    gram_rr = block_product(high_cols, high_cols)
    turns, grams = rotate_pair(gram_ll, gram_lr, gram_lr.T, gram_rr, SHIFTS)
    is_low = block_index == low_index
    coef_low = jnp.where(is_low, turns[0], turns[1])
    coef_high = jnp.where(is_low, turns[2], turns[3])
    return apply_turn(low_cols, coef_low) + apply_turn(high_cols, coef_high)

def reference(anomalies, pairing):
    block_total = MEMBERS // BLK
    current = anomalies
    for round_index in range(ROUNDS):
        pair_row = pairing[round_index]

        def one_block(block_index, current=current, pair_row=pair_row):
            return pair_output(current, pair_row, block_index)
        stacked = lax.map(one_block, jnp.arange(block_total, dtype=jnp.int32))
        current = jnp.transpose(stacked, (1, 0, 2)).reshape(SOUNDINGS, MEMBERS)
    return current
```

```python
from functools import partial

import jax
import jax.numpy as jnp
from jax import lax
from jax.experimental import pallas as pl
from jax.experimental.pallas import tpu as pltpu
from jax.sharding import PartitionSpec as P

SHIFTS = 8
TIE_GUARD = 1e-06
MESH = pl.DeviceIdType.MESH
HIGHEST = lax.Precision.HIGHEST


def dot(left, right):
    return jnp.dot(left, right, precision=HIGHEST, preferred_element_type=jnp.float32)


def dot_t(left, right):
    return lax.dot_general(
        left,
        right,
        (((0,), (0,)), ((), ())),
        precision=HIGHEST,
        preferred_element_type=jnp.float32,
    )


def exchange_kernel(count, x_ref, out_ref, send_sem, recv_sem, local_sem):
    me = lax.axis_index("cols")
    chips = count // 2
    chip = me // 2
    core = me % 2
    side = 1 - 2 * (chip // (chips // 2))

    barrier = pltpu.get_barrier_semaphore()
    for d in range(1, count):
        pl.semaphore_signal(
            barrier, inc=1, device_id={"cols": (me + d) % count}, device_id_type=MESH
        )
    local = pltpu.make_async_copy(x_ref.at[me], out_ref.at[me], local_sem)
    local.start()
    pl.semaphore_wait(barrier, count - 1)

    copies = []
    for k in [*range(1, chips), 0]:
        for flip in (0, 1):
            if k == 0 and flip == 0:
                continue
            dest_chip = (chip + side * k + chips) % chips
            dest = dest_chip * 2 + (core + flip) % 2
            copy = pltpu.make_async_remote_copy(
                src_ref=x_ref.at[dest],
                dst_ref=out_ref.at[me],
                send_sem=send_sem.at[len(copies)],
                recv_sem=recv_sem.at[me],
                device_id={"cols": dest},
                device_id_type=MESH,
            )
            copy.start()
            copies.append(copy)
    local.wait()
    for d in range(1, count):
        source = (me + d) % count
        pltpu.make_async_remote_copy(
            src_ref=x_ref.at[source],
            dst_ref=out_ref.at[source],
            send_sem=send_sem.at[0],
            recv_sem=recv_sem.at[source],
            device_id={"cols": source},
            device_id_type=MESH,
        ).wait_recv()
    for copy in copies:
        copy.wait_send()


def exchange(x, collective_id):
    count = x.shape[0]
    return pl.pallas_call(
        partial(exchange_kernel, count),
        out_shape=jax.ShapeDtypeStruct(x.shape, x.dtype),
        in_specs=[pl.BlockSpec(memory_space=pl.ANY)],
        out_specs=pl.BlockSpec(memory_space=pl.ANY),
        scratch_shapes=[
            pltpu.SemaphoreType.DMA((count - 1,)),
            pltpu.SemaphoreType.DMA((count,)),
            pltpu.SemaphoreType.DMA,
        ],
        compiler_params=pltpu.CompilerParams(
            collective_id=collective_id, has_side_effects=True
        ),
    )(x)


def quad_blocks(pairing, count):
    m0 = pairing[0, 0]
    m1 = pairing[1, 0]
    lower_mask = jnp.minimum(m0, m1)
    low_bits = jnp.int32(0)
    for bit in range(1, count.bit_length() - 1):
        low_bits = jnp.where(lower_mask >= (1 << bit), (1 << bit) - 1, low_bits)
    g = jnp.arange(count // 4, dtype=jnp.int32)
    rest = g & low_bits
    q0 = rest + 2 * (g - rest)
    return jnp.stack([q0, q0 ^ m0, q0 ^ m1, q0 ^ (count - 1)], axis=1)


def gram_kernel(quads, x_ref, gram_ref):
    g = pl.program_id(0)
    a = jnp.concatenate([x_ref[quads[g, 0]], x_ref[quads[g, 1]]], axis=1)
    b = jnp.concatenate([x_ref[quads[g, 2]], x_ref[quads[g, 3]]], axis=1)
    gram_ref[0, 0] = dot_t(a, a)
    gram_ref[0, 1] = dot_t(b, b)
    gram_ref[0, 2] = dot_t(a, b)


def gram(quads, x):
    groups = quads.shape[0]
    width = 2 * x.shape[2]
    return pl.pallas_call(
        gram_kernel,
        grid_spec=pltpu.PrefetchScalarGridSpec(
            num_scalar_prefetch=1,
            grid=(groups,),
            in_specs=[pl.BlockSpec(memory_space=pltpu.VMEM)],
            out_specs=pl.BlockSpec((1, 3, width, width), lambda g, q: (g, 0, 0, 0)),
        ),
        out_shape=jax.ShapeDtypeStruct((groups, 3, width, width), jnp.float32),
    )(quads, x)


def turn_pairs(work):
    w = work.shape[2]
    row = lax.broadcasted_iota(jnp.int32, (w, w), 0)
    col = lax.broadcasted_iota(jnp.int32, (w, w), 1)

    def diag(value):
        return jnp.sum(jnp.where(row == col, value, 0.0), axis=0, keepdims=True)

    @pl.loop(0, SHIFTS)
    def _(step):
        for p in range(2):
            g_ll, g_lr, g_rl, g_rr = (work[p, i] for i in range(4))
            a, e, g = diag(g_ll), diag(g_rr), diag(g_lr)
            gap = e - a
            sign = jnp.where(gap >= 0.0, 1.0, -1.0)
            denom = jnp.abs(gap) + jnp.sqrt(gap * gap + 4.0 * g * g) + TIE_GUARD * (a + e)
            tangent = 2.0 * g * sign / denom
            cosine = 1.0 / jnp.sqrt(1.0 + tangent * tangent)
            sine = cosine * tangent
            cc = jnp.broadcast_to(cosine, (w, w))
            ss = jnp.broadcast_to(sine, (w, w))
            rc = cc.T
            rs = ss.T
            ul = g_ll * cc - g_lr * ss
            ll = g_rl * cc - g_rr * ss
            work[p, 0] = rc * ul - rs * ll
            work[p, 2] = pltpu.roll(rs * ul + rc * ll, w - 1, 0)
            ur = g_ll * ss + g_lr * cc
            lr = g_rl * ss + g_rr * cc
            work[p, 1] = pltpu.roll(rc * ur - rs * lr, w - 1, 1)
            work[p, 3] = pltpu.roll(pltpu.roll(rs * ur + rc * lr, w - 1, 0), w - 1, 1)
            for i in (4, 6):
                v_l, v_r = work[p, i], work[p, i + 1]
                work[p, i] = v_l * cc - v_r * ss
                work[p, i + 1] = pltpu.roll(v_l * ss + v_r * cc, w - 1, 1)


def rotate_kernel(gram_ref, turn_ref, work):
    w = work.shape[2]
    eye = jnp.where(
        lax.broadcasted_iota(jnp.int32, (w, w), 0) == lax.broadcasted_iota(jnp.int32, (w, w), 1),
        1.0,
        0.0,
    )
    lo, hi = slice(0, w), slice(w, 2 * w)

    def reset_turns():
        for p in range(2):
            work[p, 4] = eye
            work[p, 5] = jnp.zeros_like(eye)
            work[p, 6] = jnp.zeros_like(eye)
            work[p, 7] = eye

    def put_turns(p, slot):
        turn_ref[0, slot, lo, lo] = work[p, 4]
        turn_ref[0, slot, lo, hi] = pltpu.roll(work[p, 5], SHIFTS, 1)
        turn_ref[0, slot, hi, lo] = work[p, 6]
        turn_ref[0, slot, hi, hi] = pltpu.roll(work[p, 7], SHIFTS, 1)

    for p in range(2):
        work[p, 0] = gram_ref[0, p, lo, lo]
        work[p, 1] = gram_ref[0, p, lo, hi]
        work[p, 2] = gram_ref[0, p, hi, lo]
        work[p, 3] = gram_ref[0, p, hi, hi]
    reset_turns()
    turn_pairs(work)
    for p in range(2):
        put_turns(p, p)

    half = dot(gram_ref[0, 2], turn_ref[0, 1])
    cross = [
        dot_t(turn_ref[0, 0, :, lo], half[:, lo]),
        dot_t(turn_ref[0, 0, :, hi], half[:, hi]),
    ]
    left = [work[0, 0], pltpu.roll(pltpu.roll(work[0, 3], SHIFTS, 0), SHIFTS, 1)]
    right = [work[1, 0], pltpu.roll(pltpu.roll(work[1, 3], SHIFTS, 0), SHIFTS, 1)]
    for p in range(2):
        work[p, 0] = left[p]
        work[p, 1] = cross[p]
        work[p, 2] = cross[p].T
        work[p, 3] = right[p]
    reset_turns()
    turn_pairs(work)
    for p in range(2):
        put_turns(p, 2 + p)


def rotate(gram_sum):
    groups, _, width, _ = gram_sum.shape
    return pl.pallas_call(
        rotate_kernel,
        grid=(groups,),
        in_specs=[pl.BlockSpec((1, 3, width, width), lambda g: (g, 0, 0, 0))],
        out_specs=pl.BlockSpec((1, 4, width, width), lambda g: (g, 0, 0, 0)),
        out_shape=jax.ShapeDtypeStruct((groups, 4, width, width), jnp.float32),
        scratch_shapes=[pltpu.VMEM((2, 8, width // 2, width // 2), jnp.float32)],
    )(gram_sum)


def apply_kernel(quads, x_ref, turn_ref, y_ref):
    g = pl.program_id(0)
    w = x_ref.shape[2]
    q = [quads[g, i] for i in range(4)]
    a = dot(jnp.concatenate([x_ref[q[0]], x_ref[q[1]]], axis=1), turn_ref[0, 0])
    b = dot(jnp.concatenate([x_ref[q[2]], x_ref[q[3]]], axis=1), turn_ref[0, 1])
    c = dot(jnp.concatenate([a[:, :w], b[:, :w]], axis=1), turn_ref[0, 2])
    d = dot(jnp.concatenate([a[:, w:], b[:, w:]], axis=1), turn_ref[0, 3])
    y_ref[q[0]] = c[:, :w]
    y_ref[q[2]] = c[:, w:]
    y_ref[q[1]] = d[:, :w]
    y_ref[q[3]] = d[:, w:]


def apply_turns(quads, x, turns):
    groups, _, width, _ = turns.shape
    return pl.pallas_call(
        apply_kernel,
        grid_spec=pltpu.PrefetchScalarGridSpec(
            num_scalar_prefetch=1,
            grid=(groups,),
            in_specs=[
                pl.BlockSpec(memory_space=pltpu.VMEM),
                pl.BlockSpec((1, 4, width, width), lambda g, q: (g, 0, 0, 0)),
            ],
            out_specs=pl.BlockSpec(memory_space=pltpu.VMEM),
        ),
        out_shape=jax.ShapeDtypeStruct(x.shape, x.dtype),
    )(quads, x, turns)


def on_device(anomalies, pairing):
    count = lax.axis_size("cols")
    rows, width = anomalies.shape
    quads = quad_blocks(pairing, count)
    x = exchange(anomalies.reshape(count, rows // count, width), 1)
    gram_sum = lax.psum(gram(quads, x), ("rows", "cols"))
    turns = rotate(gram_sum)
    y = apply_turns(quads, x, turns)
    return exchange(y, 2).reshape(rows, width)


def solution(mesh):
    placed = (P("rows", "cols"), P())
    return jax.shard_map(
        on_device, mesh=mesh, in_specs=placed, out_specs=P("rows", "cols"), check_vma=False
    )
```

```python
from functools import partial

import jax
import jax.numpy as jnp
from jax import lax
from jax.experimental import pallas as pl
from jax.experimental.pallas import tpu as pltpu
from jax.sharding import PartitionSpec as P

SHIFTS = 8
TIE_GUARD = 1e-06
BAND = 2 * SHIFTS
PAIRS = 10
MESH = pl.DeviceIdType.MESH
HIGHEST = lax.Precision.HIGHEST


def dot(left, right):
    return jnp.dot(left, right, precision=HIGHEST, preferred_element_type=jnp.float32)


def dot_t(left, right):
    return lax.dot_general(
        left,
        right,
        (((0,), (0,)), ((), ())),
        precision=HIGHEST,
        preferred_element_type=jnp.float32,
    )


def exchange_kernel(count, x_ref, out_ref, send_sem, recv_sem, local_sem):
    me = lax.axis_index("cols")
    chips = count // 2
    chip = me // 2
    core = me % 2
    side = 1 - 2 * (chip // (chips // 2))

    barrier = pltpu.get_barrier_semaphore()
    for d in range(1, count):
        pl.semaphore_signal(
            barrier, inc=1, device_id={"cols": (me + d) % count}, device_id_type=MESH
        )
    local = pltpu.make_async_copy(x_ref.at[me], out_ref.at[me], local_sem)
    local.start()
    pl.semaphore_wait(barrier, count - 1)

    copies = []
    for k in [*range(1, chips), 0]:
        for flip in (0, 1):
            if k == 0 and flip == 0:
                continue
            dest_chip = (chip + side * k + chips) % chips
            dest = dest_chip * 2 + (core + flip) % 2
            copy = pltpu.make_async_remote_copy(
                src_ref=x_ref.at[dest],
                dst_ref=out_ref.at[me],
                send_sem=send_sem.at[len(copies)],
                recv_sem=recv_sem.at[me],
                device_id={"cols": dest},
                device_id_type=MESH,
            )
            copy.start()
            copies.append(copy)
    local.wait()
    for d in range(1, count):
        source = (me + d) % count
        pltpu.make_async_remote_copy(
            src_ref=x_ref.at[source],
            dst_ref=out_ref.at[source],
            send_sem=send_sem.at[0],
            recv_sem=recv_sem.at[source],
            device_id={"cols": source},
            device_id_type=MESH,
        ).wait_recv()
    for copy in copies:
        copy.wait_send()


def exchange(x, collective_id):
    count = x.shape[0]
    return pl.pallas_call(
        partial(exchange_kernel, count),
        out_shape=jax.ShapeDtypeStruct(x.shape, x.dtype),
        in_specs=[pl.BlockSpec(memory_space=pl.ANY)],
        out_specs=pl.BlockSpec(memory_space=pl.ANY),
        scratch_shapes=[
            pltpu.SemaphoreType.DMA((count - 1,)),
            pltpu.SemaphoreType.DMA((count,)),
            pltpu.SemaphoreType.DMA,
        ],
        compiler_params=pltpu.CompilerParams(
            collective_id=collective_id, has_side_effects=True
        ),
    )(x)


def quad_blocks(pairing, count):
    m0 = pairing[0, 0]
    m1 = pairing[1, 0]
    lower_mask = jnp.minimum(m0, m1)
    low_bits = jnp.int32(0)
    for bit in range(1, count.bit_length() - 1):
        low_bits = jnp.where(lower_mask >= (1 << bit), (1 << bit) - 1, low_bits)
    g = jnp.arange(count // 4, dtype=jnp.int32)
    rest = g & low_bits
    q0 = rest + 2 * (g - rest)
    return jnp.stack([q0, q0 ^ m0, q0 ^ m1, q0 ^ (count - 1)], axis=1)


def lane_bit(shape, bit):
    return (lax.broadcasted_iota(jnp.int32, shape, 1) & (1 << bit)) != 0


def to_bands(block):
    w = block.shape[0]
    for bit in range(w.bit_length() - 1):
        block = jnp.where(
            lane_bit(block.shape, bit), pltpu.roll(block, w - (1 << bit), 0), block
        )
    return jnp.concatenate([block[w - BAND :], block[:BAND]], axis=0)


def from_bands(bands):
    w = bands.shape[1]
    block = jnp.concatenate(
        [bands[BAND:], jnp.zeros((w - 2 * BAND, w), jnp.float32), bands[:BAND]], axis=0
    )
    for bit in range(w.bit_length() - 1):
        block = jnp.where(lane_bit(block.shape, bit), pltpu.roll(block, 1 << bit, 0), block)
    return block


def gram_kernel(quads, x_ref, band_ref):
    g = pl.program_id(0)
    w = x_ref.shape[2]
    lo, hi = slice(0, w), slice(w, 2 * w)
    a = jnp.concatenate([x_ref[quads[g, 0]], x_ref[quads[g, 1]]], axis=1)
    b = jnp.concatenate([x_ref[quads[g, 2]], x_ref[quads[g, 3]]], axis=1)
    aa, bb, ba = dot_t(a, a), dot_t(b, b), dot_t(b, a)
    blocks = [aa[lo, lo], aa[hi, lo], aa[hi, hi], bb[lo, lo], bb[hi, lo], bb[hi, hi]]
    blocks += [ba[lo, lo], ba[lo, hi], ba[hi, lo], ba[hi, hi]]

    @pl.when(g == 0)
    def _():
        band_ref[...] = jnp.zeros_like(band_ref)

    for i, block in enumerate(blocks):
        start = pl.multiple_of((g * PAIRS + i) * 2 * BAND, 2 * BAND)
        band_ref[pl.ds(start, 2 * BAND), :] = to_bands(block)


def gram(quads, x, total):
    return pl.pallas_call(
        gram_kernel,
        grid_spec=pltpu.PrefetchScalarGridSpec(
            num_scalar_prefetch=1,
            grid=(quads.shape[0],),
            in_specs=[pl.BlockSpec(memory_space=pltpu.VMEM)],
            out_specs=pl.BlockSpec(memory_space=pltpu.VMEM),
        ),
        out_shape=jax.ShapeDtypeStruct((total, x.shape[2]), jnp.float32),
    )(quads, x)


def sum_kernel(x_ref, out_ref, landed, part, slots, whole, send_sem, recv_sem):
    rows, cols = x_ref.shape[0], x_ref.shape[1]
    r, c = lax.axis_index("rows"), lax.axis_index("cols")
    barrier = pltpu.get_barrier_semaphore()
    for d in range(1, rows):
        pl.semaphore_signal(barrier, inc=1, device_id={"rows": (r + d) % rows}, device_id_type=MESH)
    for d in range(1, cols):
        pl.semaphore_signal(barrier, inc=1, device_id={"cols": (c + d) % cols}, device_id_type=MESH)
    pl.semaphore_wait(barrier, rows + cols - 2)

    def stage(number, axis, me, count, source, dest):
        copies = []
        for d in range(1, count):
            peer = (me + d) % count
            copy = pltpu.make_async_remote_copy(
                src_ref=source(peer),
                dst_ref=dest(d),
                send_sem=send_sem.at[number, d],
                recv_sem=recv_sem.at[number, d],
                device_id={axis: peer},
                device_id_type=MESH,
            )
            copy.start()
            copies.append(copy)
        for copy in copies:
            copy.wait_recv()
        return copies

    def finish(copies):
        for copy in copies:
            copy.wait_send()

    sent = stage(0, "rows", r, rows, lambda p: x_ref.at[p], lambda d: landed.at[d])
    total = x_ref[r]
    for d in range(1, rows):
        total = total + landed[d]
    part[...] = total
    sent += stage(1, "cols", c, cols, lambda p: part.at[p], lambda d: slots.at[d])
    total = part[c]
    for d in range(1, cols):
        total = total + slots[d]
    whole[c] = total
    sent += stage(2, "cols", c, cols, lambda p: whole.at[c], lambda d: whole.at[c])
    out_ref[r] = whole[...]
    sent += stage(3, "rows", r, rows, lambda p: whole, lambda d: out_ref.at[r])
    finish(sent)


def sum_all(x, rows, cols):
    total, width = x.shape
    piece = total // (rows * cols)
    peers = max(rows, cols)
    summed = pl.pallas_call(
        sum_kernel,
        out_shape=jax.ShapeDtypeStruct((rows, cols, piece, width), jnp.float32),
        in_specs=[pl.BlockSpec(memory_space=pltpu.VMEM)],
        out_specs=pl.BlockSpec(memory_space=pltpu.VMEM),
        scratch_shapes=[
            pltpu.VMEM((rows, cols, piece, width), jnp.float32),
            pltpu.VMEM((cols, piece, width), jnp.float32),
            pltpu.VMEM((cols, piece, width), jnp.float32),
            pltpu.VMEM((cols, piece, width), jnp.float32),
            pltpu.SemaphoreType.DMA((4, peers)),
            pltpu.SemaphoreType.DMA((4, peers)),
        ],
        compiler_params=pltpu.CompilerParams(collective_id=3, has_side_effects=True),
    )(x.reshape(rows, cols, piece, width))
    return summed.reshape(total, width)


def turn_pairs(work):
    w = work.shape[2]
    row = lax.broadcasted_iota(jnp.int32, (w, w), 0)
    col = lax.broadcasted_iota(jnp.int32, (w, w), 1)

    def diag(value):
        return jnp.sum(jnp.where(row == col, value, 0.0), axis=0, keepdims=True)

    @pl.loop(0, SHIFTS)
    def _(step):
        for p in range(2):
            g_ll, g_lr, g_rl, g_rr = (work[p, i] for i in range(4))
            a, e, g = diag(g_ll), diag(g_rr), diag(g_lr)
            gap = e - a
            sign = jnp.where(gap >= 0.0, 1.0, -1.0)
            denom = jnp.abs(gap) + jnp.sqrt(gap * gap + 4.0 * g * g) + TIE_GUARD * (a + e)
            tangent = 2.0 * g * sign / denom
            cosine = 1.0 / jnp.sqrt(1.0 + tangent * tangent)
            sine = cosine * tangent
            cc = jnp.broadcast_to(cosine, (w, w))
            ss = jnp.broadcast_to(sine, (w, w))
            rc = cc.T
            rs = ss.T
            ul = g_ll * cc - g_lr * ss
            ll = g_rl * cc - g_rr * ss
            work[p, 0] = rc * ul - rs * ll
            work[p, 2] = pltpu.roll(rs * ul + rc * ll, w - 1, 0)
            ur = g_ll * ss + g_lr * cc
            lr = g_rl * ss + g_rr * cc
            work[p, 1] = pltpu.roll(rc * ur - rs * lr, w - 1, 1)
            work[p, 3] = pltpu.roll(pltpu.roll(rs * ur + rc * lr, w - 1, 0), w - 1, 1)
            for i in (4, 6):
                v_l, v_r = work[p, i], work[p, i + 1]
                work[p, i] = v_l * cc - v_r * ss
                work[p, i + 1] = pltpu.roll(v_l * ss + v_r * cc, w - 1, 1)


def rotate_kernel(band_ref, turn_ref, work):
    w = work.shape[2]
    eye = jnp.where(
        lax.broadcasted_iota(jnp.int32, (w, w), 0) == lax.broadcasted_iota(jnp.int32, (w, w), 1),
        1.0,
        0.0,
    )
    lo, hi = slice(0, w), slice(w, 2 * w)

    def block(i):
        return from_bands(band_ref[i * 2 * BAND : (i + 1) * 2 * BAND, :])

    def reset_turns():
        for p in range(2):
            work[p, 4] = eye
            work[p, 5] = jnp.zeros_like(eye)
            work[p, 6] = jnp.zeros_like(eye)
            work[p, 7] = eye

    def put_turns(p, slot):
        turn_ref[0, slot, lo, lo] = work[p, 4]
        turn_ref[0, slot, lo, hi] = pltpu.roll(work[p, 5], SHIFTS, 1)
        turn_ref[0, slot, hi, lo] = work[p, 6]
        turn_ref[0, slot, hi, hi] = pltpu.roll(work[p, 7], SHIFTS, 1)

    for p in range(2):
        work[p, 0] = block(3 * p)
        below = block(3 * p + 1)
        work[p, 1] = below.T
        work[p, 2] = below
        work[p, 3] = block(3 * p + 2)
    reset_turns()
    turn_pairs(work)
    for p in range(2):
        put_turns(p, p)

    cross = jnp.concatenate(
        [
            jnp.concatenate([block(6), block(7)], axis=1),
            jnp.concatenate([block(8), block(9)], axis=1),
        ],
        axis=0,
    )
    half = dot(cross, turn_ref[0, 0])
    below = [
        dot_t(turn_ref[0, 1, :, lo], half[:, lo]),
        dot_t(turn_ref[0, 1, :, hi], half[:, hi]),
    ]
    left = [work[0, 0], pltpu.roll(pltpu.roll(work[0, 3], SHIFTS, 0), SHIFTS, 1)]
    right = [work[1, 0], pltpu.roll(pltpu.roll(work[1, 3], SHIFTS, 0), SHIFTS, 1)]
    for p in range(2):
        work[p, 0] = left[p]
        work[p, 1] = below[p].T
        work[p, 2] = below[p]
        work[p, 3] = right[p]
    reset_turns()
    turn_pairs(work)
    for p in range(2):
        put_turns(p, 2 + p)


def rotate(bands, groups):
    w = bands.shape[1]
    return pl.pallas_call(
        rotate_kernel,
        grid=(groups,),
        in_specs=[pl.BlockSpec((PAIRS * 2 * BAND, w), lambda g: (g, 0))],
        out_specs=pl.BlockSpec((1, 4, 2 * w, 2 * w), lambda g: (g, 0, 0, 0)),
        out_shape=jax.ShapeDtypeStruct((groups, 4, 2 * w, 2 * w), jnp.float32),
        scratch_shapes=[pltpu.VMEM((2, 8, w, w), jnp.float32)],
    )(bands)


def apply_kernel(quads, x_ref, turn_ref, y_ref):
    g = pl.program_id(0)
    w = x_ref.shape[2]
    q = [quads[g, i] for i in range(4)]
    a = dot(jnp.concatenate([x_ref[q[0]], x_ref[q[1]]], axis=1), turn_ref[0, 0])
    b = dot(jnp.concatenate([x_ref[q[2]], x_ref[q[3]]], axis=1), turn_ref[0, 1])
    c = dot(jnp.concatenate([a[:, :w], b[:, :w]], axis=1), turn_ref[0, 2])
    d = dot(jnp.concatenate([a[:, w:], b[:, w:]], axis=1), turn_ref[0, 3])
    y_ref[q[0]] = c[:, :w]
    y_ref[q[2]] = c[:, w:]
    y_ref[q[1]] = d[:, :w]
    y_ref[q[3]] = d[:, w:]


def apply_turns(quads, x, turns):
    groups, _, width, _ = turns.shape
    return pl.pallas_call(
        apply_kernel,
        grid_spec=pltpu.PrefetchScalarGridSpec(
            num_scalar_prefetch=1,
            grid=(groups,),
            in_specs=[
                pl.BlockSpec(memory_space=pltpu.VMEM),
                pl.BlockSpec((1, 4, width, width), lambda g, q: (g, 0, 0, 0)),
            ],
            out_specs=pl.BlockSpec(memory_space=pltpu.VMEM),
        ),
        out_shape=jax.ShapeDtypeStruct(x.shape, x.dtype),
    )(quads, x, turns)


def on_device(anomalies, pairing):
    count = lax.axis_size("cols")
    rows, width = anomalies.shape
    quads = quad_blocks(pairing, count)
    x = exchange(anomalies.reshape(count, rows // count, width), 1)
    split = lax.axis_size("rows")
    groups = count // 4
    unit = 8 * split * count
    total = -(-groups * PAIRS * 2 * BAND // unit) * unit
    bands = sum_all(gram(quads, x, total), split, count)
    turns = rotate(bands, groups)
    y = apply_turns(quads, x, turns)
    return exchange(y, 2).reshape(rows, width)


def solution(mesh):
    placed = (P("rows", "cols"), P())
    return jax.shard_map(
        on_device, mesh=mesh, in_specs=placed, out_specs=P("rows", "cols"), check_vma=False
    )
```

```python
from functools import partial

import jax
import jax.numpy as jnp
from jax import lax
from jax.experimental import pallas as pl
from jax.experimental.pallas import tpu as pltpu
from jax.sharding import PartitionSpec as P

SHIFTS = 8
TIE_GUARD = 1e-06
BAND = 2 * SHIFTS
PAIRS = 10
MESH = pl.DeviceIdType.MESH
HIGHEST = lax.Precision.HIGHEST


def dot(left, right):
    return jnp.dot(left, right, precision=HIGHEST, preferred_element_type=jnp.float32)


def dot_t(left, right):
    return lax.dot_general(
        left,
        right,
        (((0,), (0,)), ((), ())),
        precision=HIGHEST,
        preferred_element_type=jnp.float32,
    )


def exchange_kernel(count, x_ref, out_ref, send_sem, recv_sem, local_sem):
    me = lax.axis_index("cols")
    chips = count // 2
    chip = me // 2
    core = me % 2
    side = 1 - 2 * (chip // (chips // 2))

    barrier = pltpu.get_barrier_semaphore()
    for d in range(1, count):
        pl.semaphore_signal(
            barrier, inc=1, device_id={"cols": (me + d) % count}, device_id_type=MESH
        )
    local = pltpu.make_async_copy(x_ref.at[me], out_ref.at[me], local_sem)
    local.start()
    pl.semaphore_wait(barrier, count - 1)

    copies = []
    for k in [*range(1, chips), 0]:
        for flip in (0, 1):
            if k == 0 and flip == 0:
                continue
            dest_chip = (chip + side * k + chips) % chips
            dest = dest_chip * 2 + (core + flip) % 2
            copy = pltpu.make_async_remote_copy(
                src_ref=x_ref.at[dest],
                dst_ref=out_ref.at[me],
                send_sem=send_sem.at[len(copies)],
                recv_sem=recv_sem.at[me],
                device_id={"cols": dest},
                device_id_type=MESH,
            )
            copy.start()
            copies.append(copy)
    local.wait()
    for d in range(1, count):
        source = (me + d) % count
        pltpu.make_async_remote_copy(
            src_ref=x_ref.at[source],
            dst_ref=out_ref.at[source],
            send_sem=send_sem.at[0],
            recv_sem=recv_sem.at[source],
            device_id={"cols": source},
            device_id_type=MESH,
        ).wait_recv()
    for copy in copies:
        copy.wait_send()


def exchange(x, collective_id):
    count = x.shape[0]
    return pl.pallas_call(
        partial(exchange_kernel, count),
        out_shape=jax.ShapeDtypeStruct(x.shape, x.dtype),
        in_specs=[pl.BlockSpec(memory_space=pl.ANY)],
        out_specs=pl.BlockSpec(memory_space=pl.ANY),
        scratch_shapes=[
            pltpu.SemaphoreType.DMA((count - 1,)),
            pltpu.SemaphoreType.DMA((count,)),
            pltpu.SemaphoreType.DMA,
        ],
        compiler_params=pltpu.CompilerParams(
            collective_id=collective_id, has_side_effects=True
        ),
    )(x)


def quad_blocks(pairing, count, g):
    m0 = pairing[0, 0]
    m1 = pairing[1, 0]
    lower_mask = jnp.minimum(m0, m1)
    low_bits = jnp.int32(0)
    for bit in range(1, count.bit_length() - 1):
        low_bits = jnp.where(lower_mask >= (1 << bit), (1 << bit) - 1, low_bits)
    rest = g & low_bits
    q0 = rest + 2 * (g - rest)
    return q0, q0 ^ m0, q0 ^ m1, q0 ^ (count - 1)


def lane_bit(shape, bit):
    return (lax.broadcasted_iota(jnp.int32, shape, 1) & (1 << bit)) != 0


def to_bands(block):
    w = block.shape[0]
    for bit in range(w.bit_length() - 1):
        block = jnp.where(
            lane_bit(block.shape, bit), pltpu.roll(block, w - (1 << bit), 0), block
        )
    return jnp.concatenate([block[w - BAND :], block[:BAND]], axis=0)


def from_bands(bands):
    w = bands.shape[1]
    block = jnp.concatenate(
        [bands[BAND:], jnp.zeros((w - 2 * BAND, w), jnp.float32), bands[:BAND]], axis=0
    )
    for bit in range(w.bit_length() - 1):
        block = jnp.where(lane_bit(block.shape, bit), pltpu.roll(block, 1 << bit, 0), block)
    return block


def gram_kernel(pairing, x_ref, band_ref):
    g = pl.program_id(0)
    q = quad_blocks(pairing, x_ref.shape[0], g)
    w = x_ref.shape[2]
    lo, hi = slice(0, w), slice(w, 2 * w)
    a = jnp.concatenate([x_ref[q[0]], x_ref[q[1]]], axis=1)
    b = jnp.concatenate([x_ref[q[2]], x_ref[q[3]]], axis=1)
    aa, bb, ba = dot_t(a, a), dot_t(b, b), dot_t(b, a)
    blocks = [aa[lo, lo], aa[hi, lo], aa[hi, hi], bb[lo, lo], bb[hi, lo], bb[hi, hi]]
    blocks += [ba[lo, lo], ba[lo, hi], ba[hi, lo], ba[hi, hi]]

    @pl.when(g == 0)
    def _():
        band_ref[...] = jnp.zeros_like(band_ref)

    for i, block in enumerate(blocks):
        start = pl.multiple_of((g * PAIRS + i) * 2 * BAND, 2 * BAND)
        band_ref[pl.ds(start, 2 * BAND), :] = to_bands(block)


def gram(pairing, x, total):
    return pl.pallas_call(
        gram_kernel,
        grid_spec=pltpu.PrefetchScalarGridSpec(
            num_scalar_prefetch=1,
            grid=(x.shape[0] // 4,),
            in_specs=[pl.BlockSpec(memory_space=pltpu.VMEM)],
            out_specs=pl.BlockSpec(memory_space=pltpu.VMEM),
        ),
        out_shape=jax.ShapeDtypeStruct((total, x.shape[2]), jnp.float32),
    )(pairing, x)


def sum_kernel(x_ref, out_ref, landed, part, slots, whole, send_sem, recv_sem):
    rows, cols = x_ref.shape[0], x_ref.shape[1]
    r, c = lax.axis_index("rows"), lax.axis_index("cols")
    barrier = pltpu.get_barrier_semaphore()
    for d in range(1, rows):
        pl.semaphore_signal(barrier, inc=1, device_id={"rows": (r + d) % rows}, device_id_type=MESH)
    for d in range(1, cols):
        pl.semaphore_signal(barrier, inc=1, device_id={"cols": (c + d) % cols}, device_id_type=MESH)
    pl.semaphore_wait(barrier, rows + cols - 2)

    def stage(number, axis, me, count, source, dest):
        copies = []
        for d in range(1, count):
            peer = (me + d) % count
            copy = pltpu.make_async_remote_copy(
                src_ref=source(peer),
                dst_ref=dest(d),
                send_sem=send_sem.at[number, d],
                recv_sem=recv_sem.at[number, d],
                device_id={axis: peer},
                device_id_type=MESH,
            )
            copy.start()
            copies.append(copy)
        for copy in copies:
            copy.wait_recv()
        return copies

    def finish(copies):
        for copy in copies:
            copy.wait_send()

    sent = stage(0, "rows", r, rows, lambda p: x_ref.at[p], lambda d: landed.at[d])
    total = x_ref[r]
    for d in range(1, rows):
        total = total + landed[d]
    part[...] = total
    sent += stage(1, "cols", c, cols, lambda p: part.at[p], lambda d: slots.at[d])
    total = part[c]
    for d in range(1, cols):
        total = total + slots[d]
    whole[c] = total
    sent += stage(2, "cols", c, cols, lambda p: whole.at[c], lambda d: whole.at[c])
    out_ref[r] = whole[...]
    sent += stage(3, "rows", r, rows, lambda p: whole, lambda d: out_ref.at[r])
    finish(sent)


def sum_all(x, rows, cols):
    total, width = x.shape
    piece = total // (rows * cols)
    peers = max(rows, cols)
    summed = pl.pallas_call(
        sum_kernel,
        out_shape=jax.ShapeDtypeStruct((rows, cols, piece, width), jnp.float32),
        in_specs=[pl.BlockSpec(memory_space=pltpu.VMEM)],
        out_specs=pl.BlockSpec(memory_space=pltpu.VMEM),
        scratch_shapes=[
            pltpu.VMEM((rows, cols, piece, width), jnp.float32),
            pltpu.VMEM((cols, piece, width), jnp.float32),
            pltpu.VMEM((cols, piece, width), jnp.float32),
            pltpu.VMEM((cols, piece, width), jnp.float32),
            pltpu.SemaphoreType.DMA((4, peers)),
            pltpu.SemaphoreType.DMA((4, peers)),
        ],
        compiler_params=pltpu.CompilerParams(collective_id=3, has_side_effects=True),
    )(x.reshape(rows, cols, piece, width))
    return summed.reshape(total, width)


def turn_pairs(gram, turn, pairs):
    _, depth, sides, w = gram.shape

    def lane(value):
        return pltpu.roll(value.reshape(depth * sides, w), w - 1, 1).reshape(depth, sides, w)

    def later(value):
        return jnp.concatenate([value[-1:], value[:-1]], axis=0)

    def sooner(value):
        return jnp.concatenate([value[1:], value[:1]], axis=0)

    def swap(value):
        return jnp.concatenate([value[:, pairs:], value[:, :pairs]], axis=1)

    def ahead(value):
        return jnp.stack([pltpu.roll(value, (BAND - r) % w, 1) if r != BAND else value for r in range(depth)])

    lower = lax.broadcasted_iota(jnp.int32, (depth, sides, w), 1) >= pairs

    @pl.loop(0, SHIFTS)
    def _(step):
        g_l, g_r = gram[0], gram[1]
        a, e, g = gram[0, BAND, :pairs], gram[1, BAND, pairs:], gram[1, BAND, :pairs]
        gap = e - a
        sign = jnp.where(gap >= 0.0, 1.0, -1.0)
        denom = jnp.abs(gap) + jnp.sqrt(gap * gap + 4.0 * g * g) + TIE_GUARD * (a + e)
        tangent = 2.0 * g * sign / denom
        cosine = 1.0 / jnp.sqrt(1.0 + tangent * tangent)
        sine = cosine * tangent
        c_2 = jnp.concatenate([cosine, cosine], axis=0)
        s_2 = jnp.concatenate([sine, sine], axis=0)
        c_d = ahead(c_2)
        s_d = ahead(jnp.concatenate([-sine, sine], axis=0))
        t_l = g_l * c_2 - g_r * s_2
        t_r = g_l * s_2 + g_r * c_2
        t_l = c_d * t_l + s_d * swap(t_l)
        t_r = lane(c_d * t_r + s_d * swap(t_r))
        gram[0] = jnp.where(lower, sooner(t_l), t_l)
        gram[1] = jnp.where(lower, t_r, later(t_r))
        v_l, v_r = turn[0], turn[1]
        turn[0] = v_l * c_2 - v_r * s_2
        turn[1] = later(lane(v_l * s_2 + v_r * c_2))


def rotate_kernel(groups, band_ref, turn_ref, gram, turn):
    w = band_ref.shape[1]
    pairs = 2 * groups
    lo, hi = slice(0, w), slice(w, 2 * w)

    def bands(g, i):
        start = (g * PAIRS + i) * 2 * BAND
        return band_ref[start : start + 2 * BAND, :]

    def reset_turns():
        shape = turn.shape
        one = lax.broadcasted_iota(jnp.int32, shape, 1) == BAND
        lower = lax.broadcasted_iota(jnp.int32, shape, 2) >= pairs
        right = lax.broadcasted_iota(jnp.int32, shape, 0) == 1
        turn[...] = jnp.where(one & (lower == right), 1.0, 0.0)

    def put_turns(slot):
        for g in range(groups):
            for p in range(2):
                at = 2 * g + p
                for row, side in ((lo, at), (hi, pairs + at)):
                    turn_ref[g, slot + p, row, lo] = from_bands(turn[0, :, side, :])
                    moved = from_bands(turn[1, :, side, :])
                    turn_ref[g, slot + p, row, hi] = pltpu.roll(moved, SHIFTS, 1)

    def put_gram(at, ll, lr, rl, rr):
        gram[0, :, at, :] = ll
        gram[1, :, at, :] = lr
        gram[0, :, pairs + at, :] = rl
        gram[1, :, pairs + at, :] = rr

    for g in range(groups):
        for p in range(2):
            below = bands(g, 3 * p + 1)
            above = to_bands(from_bands(below).T)
            put_gram(2 * g + p, bands(g, 3 * p), above, below, bands(g, 3 * p + 2))
    reset_turns()
    turn_pairs(gram, turn, pairs)
    put_turns(0)

    for g in range(groups):
        blocks = [from_bands(bands(g, 6 + i)) for i in range(4)]
        cross = jnp.concatenate(
            [
                jnp.concatenate([blocks[0], blocks[1]], axis=1),
                jnp.concatenate([blocks[2], blocks[3]], axis=1),
            ],
            axis=0,
        )
        half = dot(cross, turn_ref[g, 0])
        below = [
            dot_t(turn_ref[g, 1, :, lo], half[:, lo]),
            dot_t(turn_ref[g, 1, :, hi], half[:, hi]),
        ]
        a, b = 2 * g, 2 * g + 1
        a_lo, b_lo = gram[0, :, a, :], gram[0, :, b, :]
        a_hi = pltpu.roll(gram[1, :, pairs + a, :], SHIFTS, 1)
        b_hi = pltpu.roll(gram[1, :, pairs + b, :], SHIFTS, 1)
        put_gram(a, a_lo, to_bands(below[0].T), to_bands(below[0]), b_lo)
        put_gram(b, a_hi, to_bands(below[1].T), to_bands(below[1]), b_hi)
    reset_turns()
    turn_pairs(gram, turn, pairs)
    put_turns(2)


def rotate(bands, groups):
    w = bands.shape[1]
    state = pltpu.VMEM((2, 2 * BAND, 4 * groups, w), jnp.float32)
    return pl.pallas_call(
        partial(rotate_kernel, groups),
        in_specs=[pl.BlockSpec(memory_space=pltpu.VMEM)],
        out_specs=pl.BlockSpec(memory_space=pltpu.VMEM),
        out_shape=jax.ShapeDtypeStruct((groups, 4, 2 * w, 2 * w), jnp.float32),
        scratch_shapes=[state, state],
    )(bands)


def apply_kernel(pairing, x_ref, turn_ref, y_ref):
    g = pl.program_id(0)
    w = x_ref.shape[2]
    q = quad_blocks(pairing, x_ref.shape[0], g)
    a = dot(jnp.concatenate([x_ref[q[0]], x_ref[q[1]]], axis=1), turn_ref[0, 0])
    b = dot(jnp.concatenate([x_ref[q[2]], x_ref[q[3]]], axis=1), turn_ref[0, 1])
    c = dot(jnp.concatenate([a[:, :w], b[:, :w]], axis=1), turn_ref[0, 2])
    d = dot(jnp.concatenate([a[:, w:], b[:, w:]], axis=1), turn_ref[0, 3])
    y_ref[q[0]] = c[:, :w]
    y_ref[q[2]] = c[:, w:]
    y_ref[q[1]] = d[:, :w]
    y_ref[q[3]] = d[:, w:]


def apply_turns(pairing, x, turns):
    groups, _, width, _ = turns.shape
    return pl.pallas_call(
        apply_kernel,
        grid_spec=pltpu.PrefetchScalarGridSpec(
            num_scalar_prefetch=1,
            grid=(groups,),
            in_specs=[
                pl.BlockSpec(memory_space=pltpu.VMEM),
                pl.BlockSpec((1, 4, width, width), lambda g, q: (g, 0, 0, 0)),
            ],
            out_specs=pl.BlockSpec(memory_space=pltpu.VMEM),
        ),
        out_shape=jax.ShapeDtypeStruct(x.shape, x.dtype),
    )(pairing, x, turns)


def on_device(anomalies, pairing):
    count = lax.axis_size("cols")
    rows, width = anomalies.shape
    x = exchange(anomalies.reshape(count, rows // count, width), 1)
    split = lax.axis_size("rows")
    groups = count // 4
    unit = 8 * split * count
    total = -(-groups * PAIRS * 2 * BAND // unit) * unit
    bands = sum_all(gram(pairing, x, total), split, count)
    turns = rotate(bands, groups)
    y = apply_turns(pairing, x, turns)
    return exchange(y, 2).reshape(rows, width)


def solution(mesh):
    placed = (P("rows", "cols"), P())
    return jax.shard_map(
        on_device, mesh=mesh, in_specs=placed, out_specs=P("rows", "cols"), check_vma=False
    )
```

```python
from functools import partial

import jax
import jax.numpy as jnp
from jax import lax
from jax.experimental import pallas as pl
from jax.experimental.pallas import tpu as pltpu
from jax.sharding import PartitionSpec as P

SHIFTS = 8
TIE_GUARD = 1e-06
BAND = 2 * SHIFTS
PAIRS = 10
MESH = pl.DeviceIdType.MESH
HIGHEST = lax.Precision.HIGHEST


def dot(left, right):
    return jnp.dot(left, right, precision=HIGHEST, preferred_element_type=jnp.float32)


def dot_t(left, right):
    return lax.dot_general(
        left,
        right,
        (((0,), (0,)), ((), ())),
        precision=HIGHEST,
        preferred_element_type=jnp.float32,
    )


def exchange_kernel(count, make_piece, out_ref, send_sem, recv_sem, local_sem):
    me = lax.axis_index("cols")
    chips = count // 2
    chip = me // 2
    core = me % 2
    side = 1 - 2 * (chip // (chips // 2))

    barrier = pltpu.get_barrier_semaphore()
    for d in range(1, count):
        pl.semaphore_signal(
            barrier, inc=1, device_id={"cols": (me + d) % count}, device_id_type=MESH
        )
    copies = []
    for k in [*range(1, chips), 0]:
        for flip in (0, 1):
            if k == 0 and flip == 0:
                continue
            dest_chip = (chip + side * k + chips) % chips
            dest = dest_chip * 2 + (core + flip) % 2
            piece = make_piece(len(copies), dest)
            if not copies:
                pl.semaphore_wait(barrier, count - 1)
            copy = pltpu.make_async_remote_copy(
                src_ref=piece,
                dst_ref=out_ref.at[me],
                send_sem=send_sem.at[len(copies)],
                recv_sem=recv_sem.at[me],
                device_id={"cols": dest},
                device_id_type=MESH,
            )
            copy.start()
            copies.append(copy)
    local = pltpu.make_async_copy(make_piece(count - 1, me), out_ref.at[me], local_sem)
    local.start()
    local.wait()
    for d in range(1, count):
        source = (me + d) % count
        pltpu.make_async_remote_copy(
            src_ref=copies[0].src_ref,
            dst_ref=out_ref.at[source],
            send_sem=send_sem.at[0],
            recv_sem=recv_sem.at[source],
            device_id={"cols": source},
            device_id_type=MESH,
        ).wait_recv()
    for copy in copies:
        copy.wait_send()


def gather_kernel(count, x_ref, out_ref, *sems):
    exchange_kernel(count, lambda i, dest: x_ref.at[dest], out_ref, *sems)


def halves(value):
    high = value.astype(jnp.bfloat16)
    return high, (value - high.astype(jnp.float32)).astype(jnp.bfloat16)


def dot_3(left, right):
    a, b = halves(left)
    c, d = halves(right)
    product = partial(jnp.dot, preferred_element_type=jnp.float32)
    return product(a, c) + (product(a, d) + product(b, c))


def return_kernel(count, pairing, x_ref, coef_ref, out_ref, piece_ref, *sems):
    masks = (pairing[0, 0], pairing[1, 0], count - 1)

    def make_piece(i, dest):
        blocks = [x_ref[dest]] + [x_ref[dest ^ mask] for mask in masks]
        piece_ref[i] = dot_3(jnp.concatenate(blocks, axis=1), coef_ref[dest])
        return piece_ref.at[i]

    exchange_kernel(count, make_piece, out_ref, *sems)


def exchange_sems(count):
    return [
        pltpu.SemaphoreType.DMA((count - 1,)),
        pltpu.SemaphoreType.DMA((count,)),
        pltpu.SemaphoreType.DMA,
    ]


def turn_and_return(pairing, x, coef):
    count = x.shape[0]
    return pl.pallas_call(
        partial(return_kernel, count),
        out_shape=jax.ShapeDtypeStruct(x.shape, x.dtype),
        in_specs=[
            pl.BlockSpec(memory_space=pltpu.SMEM),
            pl.BlockSpec(memory_space=pltpu.VMEM),
            pl.BlockSpec(memory_space=pltpu.VMEM),
        ],
        out_specs=pl.BlockSpec(memory_space=pl.ANY),
        scratch_shapes=[pltpu.VMEM(x.shape, x.dtype), *exchange_sems(count)],
        compiler_params=pltpu.CompilerParams(collective_id=2, has_side_effects=True),
    )(pairing, x, coef)


def exchange(x, collective_id):
    count = x.shape[0]
    return pl.pallas_call(
        partial(gather_kernel, count),
        out_shape=jax.ShapeDtypeStruct(x.shape, x.dtype),
        in_specs=[pl.BlockSpec(memory_space=pl.ANY)],
        out_specs=pl.BlockSpec(memory_space=pl.ANY),
        scratch_shapes=exchange_sems(count),
        compiler_params=pltpu.CompilerParams(
            collective_id=collective_id, has_side_effects=True
        ),
    )(x)


def quad_blocks(pairing, count, g):
    m0 = pairing[0, 0]
    m1 = pairing[1, 0]
    lower_mask = jnp.minimum(m0, m1)
    low_bits = jnp.int32(0)
    for bit in range(1, count.bit_length() - 1):
        low_bits = jnp.where(lower_mask >= (1 << bit), (1 << bit) - 1, low_bits)
    rest = g & low_bits
    q0 = rest + 2 * (g - rest)
    return q0, q0 ^ m0, q0 ^ m1, q0 ^ (count - 1)


def lane_bit(shape, bit):
    return (lax.broadcasted_iota(jnp.int32, shape, 1) & (1 << bit)) != 0


def to_bands(block):
    w = block.shape[0]
    for bit in range(w.bit_length() - 1):
        block = jnp.where(
            lane_bit(block.shape, bit), pltpu.roll(block, w - (1 << bit), 0), block
        )
    return jnp.concatenate([block[w - BAND :], block[:BAND]], axis=0)


def from_bands(bands):
    w = bands.shape[1]
    block = jnp.concatenate(
        [bands[BAND:], jnp.zeros((w - 2 * BAND, w), jnp.float32), bands[:BAND]], axis=0
    )
    for bit in range(w.bit_length() - 1):
        block = jnp.where(lane_bit(block.shape, bit), pltpu.roll(block, 1 << bit, 0), block)
    return block


def gram_kernel(pairing, x_ref, band_ref):
    g = pl.program_id(0)
    q = quad_blocks(pairing, x_ref.shape[0], g)
    w = x_ref.shape[2]
    lo, hi = slice(0, w), slice(w, 2 * w)
    a = jnp.concatenate([x_ref[q[0]], x_ref[q[1]]], axis=1)
    b = jnp.concatenate([x_ref[q[2]], x_ref[q[3]]], axis=1)
    aa, bb, ba = dot_t(a, a), dot_t(b, b), dot_t(b, a)
    blocks = [aa[lo, lo], aa[hi, lo], aa[hi, hi], bb[lo, lo], bb[hi, lo], bb[hi, hi]]
    blocks += [ba[lo, lo], ba[lo, hi], ba[hi, lo], ba[hi, hi]]

    @pl.when(g == 0)
    def _():
        band_ref[...] = jnp.zeros_like(band_ref)

    for i, block in enumerate(blocks):
        start = pl.multiple_of((g * PAIRS + i) * 2 * BAND, 2 * BAND)
        band_ref[pl.ds(start, 2 * BAND), :] = to_bands(block)


def gram(pairing, x, total):
    return pl.pallas_call(
        gram_kernel,
        grid_spec=pltpu.PrefetchScalarGridSpec(
            num_scalar_prefetch=1,
            grid=(x.shape[0] // 4,),
            in_specs=[pl.BlockSpec(memory_space=pltpu.VMEM)],
            out_specs=pl.BlockSpec(memory_space=pltpu.VMEM),
        ),
        out_shape=jax.ShapeDtypeStruct((total, x.shape[2]), jnp.float32),
    )(pairing, x)


def sum_kernel(x_ref, out_ref, landed, part, slots, whole, send_sem, recv_sem):
    rows, cols = x_ref.shape[0], x_ref.shape[1]
    r, c = lax.axis_index("rows"), lax.axis_index("cols")
    barrier = pltpu.get_barrier_semaphore()
    for d in range(1, rows):
        pl.semaphore_signal(barrier, inc=1, device_id={"rows": (r + d) % rows}, device_id_type=MESH)
    for d in range(1, cols):
        pl.semaphore_signal(barrier, inc=1, device_id={"cols": (c + d) % cols}, device_id_type=MESH)
    pl.semaphore_wait(barrier, rows + cols - 2)

    def stage(number, axis, me, count, source, dest):
        copies = []
        for d in range(1, count):
            peer = (me + d) % count
            copy = pltpu.make_async_remote_copy(
                src_ref=source(peer),
                dst_ref=dest(d),
                send_sem=send_sem.at[number, d],
                recv_sem=recv_sem.at[number, d],
                device_id={axis: peer},
                device_id_type=MESH,
            )
            copy.start()
            copies.append(copy)
        for copy in copies:
            copy.wait_recv()
        return copies

    def finish(copies):
        for copy in copies:
            copy.wait_send()

    sent = stage(0, "rows", r, rows, lambda p: x_ref.at[p], lambda d: landed.at[d])
    total = x_ref[r]
    for d in range(1, rows):
        total = total + landed[d]
    part[...] = total
    sent += stage(1, "cols", c, cols, lambda p: part.at[p], lambda d: slots.at[d])
    total = part[c]
    for d in range(1, cols):
        total = total + slots[d]
    whole[c] = total
    sent += stage(2, "cols", c, cols, lambda p: whole.at[c], lambda d: whole.at[c])
    out_ref[r] = whole[...]
    sent += stage(3, "rows", r, rows, lambda p: whole, lambda d: out_ref.at[r])
    finish(sent)


def sum_all(x, rows, cols):
    total, width = x.shape
    piece = total // (rows * cols)
    peers = max(rows, cols)
    summed = pl.pallas_call(
        sum_kernel,
        out_shape=jax.ShapeDtypeStruct((rows, cols, piece, width), jnp.float32),
        in_specs=[pl.BlockSpec(memory_space=pltpu.VMEM)],
        out_specs=pl.BlockSpec(memory_space=pltpu.VMEM),
        scratch_shapes=[
            pltpu.VMEM((rows, cols, piece, width), jnp.float32),
            pltpu.VMEM((cols, piece, width), jnp.float32),
            pltpu.VMEM((cols, piece, width), jnp.float32),
            pltpu.VMEM((cols, piece, width), jnp.float32),
            pltpu.SemaphoreType.DMA((4, peers)),
            pltpu.SemaphoreType.DMA((4, peers)),
        ],
        compiler_params=pltpu.CompilerParams(collective_id=3, has_side_effects=True),
    )(x.reshape(rows, cols, piece, width))
    return summed.reshape(total, width)


def turn_pairs(gram, turn, pairs):
    _, depth, sides, w = gram.shape

    def lane(value):
        return pltpu.roll(value.reshape(depth * sides, w), w - 1, 1).reshape(depth, sides, w)

    def later(value):
        return jnp.concatenate([value[-1:], value[:-1]], axis=0)

    def sooner(value):
        return jnp.concatenate([value[1:], value[:1]], axis=0)

    def swap(value):
        return jnp.concatenate([value[:, pairs:], value[:, :pairs]], axis=1)

    def ahead(value):
        return jnp.stack([pltpu.roll(value, (BAND - r) % w, 1) if r != BAND else value for r in range(depth)])

    lower = lax.broadcasted_iota(jnp.int32, (depth, sides, w), 1) >= pairs

    @pl.loop(0, SHIFTS)
    def _(step):
        g_l, g_r = gram[0], gram[1]
        a, e, g = gram[0, BAND, :pairs], gram[1, BAND, pairs:], gram[1, BAND, :pairs]
        gap = e - a
        sign = jnp.where(gap >= 0.0, 1.0, -1.0)
        denom = jnp.abs(gap) + jnp.sqrt(gap * gap + 4.0 * g * g) + TIE_GUARD * (a + e)
        tangent = 2.0 * g * sign / denom
        cosine = 1.0 / jnp.sqrt(1.0 + tangent * tangent)
        sine = cosine * tangent
        c_2 = jnp.concatenate([cosine, cosine], axis=0)
        s_2 = jnp.concatenate([sine, sine], axis=0)
        c_d = ahead(c_2)
        s_d = ahead(jnp.concatenate([-sine, sine], axis=0))
        t_l = g_l * c_2 - g_r * s_2
        t_r = g_l * s_2 + g_r * c_2
        t_l = c_d * t_l + s_d * swap(t_l)
        t_r = lane(c_d * t_r + s_d * swap(t_r))
        gram[0] = jnp.where(lower, sooner(t_l), t_l)
        gram[1] = jnp.where(lower, t_r, later(t_r))
        v_l, v_r = turn[0], turn[1]
        turn[0] = v_l * c_2 - v_r * s_2
        turn[1] = later(lane(v_l * s_2 + v_r * c_2))


def rotate_kernel(groups, pairing, band_ref, coef_ref, turn_ref, gram, turn):
    w = band_ref.shape[1]
    pairs = 2 * groups
    lo, hi = slice(0, w), slice(w, 2 * w)

    def bands(g, i):
        start = (g * PAIRS + i) * 2 * BAND
        return band_ref[start : start + 2 * BAND, :]

    def reset_turns():
        shape = turn.shape
        one = lax.broadcasted_iota(jnp.int32, shape, 1) == BAND
        lower = lax.broadcasted_iota(jnp.int32, shape, 2) >= pairs
        right = lax.broadcasted_iota(jnp.int32, shape, 0) == 1
        turn[...] = jnp.where(one & (lower == right), 1.0, 0.0)

    def put_turns(slot):
        for g in range(groups):
            for p in range(2):
                at = 2 * g + p
                for row, side in ((lo, at), (hi, pairs + at)):
                    turn_ref[g, slot + p, row, lo] = from_bands(turn[0, :, side, :])
                    moved = from_bands(turn[1, :, side, :])
                    turn_ref[g, slot + p, row, hi] = pltpu.roll(moved, SHIFTS, 1)

    def put_gram(at, ll, lr, rl, rr):
        gram[0, :, at, :] = ll
        gram[1, :, at, :] = lr
        gram[0, :, pairs + at, :] = rl
        gram[1, :, pairs + at, :] = rr

    for g in range(groups):
        for p in range(2):
            below = bands(g, 3 * p + 1)
            above = to_bands(from_bands(below).T)
            put_gram(2 * g + p, bands(g, 3 * p), above, below, bands(g, 3 * p + 2))
    reset_turns()
    turn_pairs(gram, turn, pairs)
    put_turns(0)

    for g in range(groups):
        blocks = [from_bands(bands(g, 6 + i)) for i in range(4)]
        cross = jnp.concatenate(
            [
                jnp.concatenate([blocks[0], blocks[1]], axis=1),
                jnp.concatenate([blocks[2], blocks[3]], axis=1),
            ],
            axis=0,
        )
        half = dot(cross, turn_ref[g, 0])
        below = [
            dot_t(turn_ref[g, 1, :, lo], half[:, lo]),
            dot_t(turn_ref[g, 1, :, hi], half[:, hi]),
        ]
        a, b = 2 * g, 2 * g + 1
        a_lo, b_lo = gram[0, :, a, :], gram[0, :, b, :]
        a_hi = pltpu.roll(gram[1, :, pairs + a, :], SHIFTS, 1)
        b_hi = pltpu.roll(gram[1, :, pairs + b, :], SHIFTS, 1)
        put_gram(a, a_lo, to_bands(below[0].T), to_bands(below[0]), b_lo)
        put_gram(b, a_hi, to_bands(below[1].T), to_bands(below[1]), b_hi)
    reset_turns()
    turn_pairs(gram, turn, pairs)
    put_turns(2)

    for g in range(groups):
        q = quad_blocks(pairing, 4 * groups, g)
        for side, part in ((0, lo), (1, hi)):
            last = turn_ref.at[g, 2 + side]
            top = dot(turn_ref[g, 0, :, part], last[lo, :])
            bottom = dot(turn_ref[g, 1, :, part], last[hi, :])
            rows = [top[lo], top[hi], bottom[lo], bottom[hi]]
            for member, cols in ((side, lo), (2 + side, hi)):
                for i in range(4):
                    coef_ref[q[member], i * w : (i + 1) * w, :] = rows[member ^ i][:, cols]


def rotate(pairing, bands, groups):
    w = bands.shape[1]
    state = pltpu.VMEM((2, 2 * BAND, 4 * groups, w), jnp.float32)
    return pl.pallas_call(
        partial(rotate_kernel, groups),
        in_specs=[
            pl.BlockSpec(memory_space=pltpu.SMEM),
            pl.BlockSpec(memory_space=pltpu.VMEM),
        ],
        out_specs=pl.BlockSpec(memory_space=pltpu.VMEM),
        out_shape=jax.ShapeDtypeStruct((4 * groups, 4 * w, w), jnp.float32),
        scratch_shapes=[
            pltpu.VMEM((groups, 4, 2 * w, 2 * w), jnp.float32),
            state,
            state,
        ],
    )(pairing, bands)


def on_device(anomalies, pairing):
    count = lax.axis_size("cols")
    rows, width = anomalies.shape
    x = exchange(anomalies.reshape(count, rows // count, width), 1)
    split = lax.axis_size("rows")
    groups = count // 4
    unit = 8 * split * count
    total = -(-groups * PAIRS * 2 * BAND // unit) * unit
    bands = sum_all(gram(pairing, x, total), split, count)
    coef = rotate(pairing, bands, groups)
    return turn_and_return(pairing, x, coef).reshape(rows, width)


def solution(mesh):
    placed = (P("rows", "cols"), P())
    return jax.shard_map(
        on_device, mesh=mesh, in_specs=placed, out_specs=P("rows", "cols"), check_vma=False
    )
```

```python
from functools import partial

import jax
import jax.numpy as jnp
from jax import lax
from jax.experimental import pallas as pl
from jax.experimental.pallas import tpu as pltpu
from jax.sharding import PartitionSpec as P

SHIFTS = 8
TIE_GUARD = 1e-06
BAND = 2 * SHIFTS
PAIRS = 10
MESH = pl.DeviceIdType.MESH
HIGHEST = lax.Precision.HIGHEST


def dot(left, right):
    return jnp.dot(left, right, precision=HIGHEST, preferred_element_type=jnp.float32)


def dot_t(left, right):
    return lax.dot_general(
        left,
        right,
        (((0,), (0,)), ((), ())),
        precision=HIGHEST,
        preferred_element_type=jnp.float32,
    )


def exchange_kernel(count, make_piece, out_ref, send_sem, recv_sem, local_sem):
    me = lax.axis_index("cols")
    chips = count // 2
    chip = me // 2
    core = me % 2
    side = 1 - 2 * (chip // (chips // 2))

    barrier = pltpu.get_barrier_semaphore()
    for d in range(1, count):
        pl.semaphore_signal(
            barrier, inc=1, device_id={"cols": (me + d) % count}, device_id_type=MESH
        )
    copies = []
    for k in [*range(1, chips), 0]:
        for flip in (0, 1):
            if k == 0 and flip == 0:
                continue
            dest_chip = (chip + side * k + chips) % chips
            dest = dest_chip * 2 + (core + flip) % 2
            piece = make_piece(len(copies), dest)
            if not copies:
                pl.semaphore_wait(barrier, count - 1)
            copy = pltpu.make_async_remote_copy(
                src_ref=piece,
                dst_ref=out_ref.at[me],
                send_sem=send_sem.at[len(copies)],
                recv_sem=recv_sem.at[me],
                device_id={"cols": dest},
                device_id_type=MESH,
            )
            copy.start()
            copies.append(copy)
    local = pltpu.make_async_copy(make_piece(count - 1, me), out_ref.at[me], local_sem)
    local.start()
    local.wait()
    for d in range(1, count):
        source = (me + d) % count
        pltpu.make_async_remote_copy(
            src_ref=copies[0].src_ref,
            dst_ref=out_ref.at[source],
            send_sem=send_sem.at[0],
            recv_sem=recv_sem.at[source],
            device_id={"cols": source},
            device_id_type=MESH,
        ).wait_recv()
    for copy in copies:
        copy.wait_send()


def gather_kernel(count, x_ref, out_ref, *sems):
    exchange_kernel(count, lambda i, dest: x_ref.at[dest], out_ref, *sems)


def halves(value):
    high = value.astype(jnp.bfloat16)
    return high, (value - high.astype(jnp.float32)).astype(jnp.bfloat16)


def dot_3(left, right):
    a, b = halves(left)
    c, d = halves(right)
    product = partial(jnp.dot, preferred_element_type=jnp.float32)
    return product(a, c) + (product(a, d) + product(b, c))


def return_kernel(count, pairing, x_ref, coef_ref, out_ref, piece_ref, *sems):
    masks = (pairing[0, 0], pairing[1, 0], count - 1)

    def make_piece(i, dest):
        blocks = [x_ref[dest]] + [x_ref[dest ^ mask] for mask in masks]
        piece_ref[i] = dot_3(jnp.concatenate(blocks, axis=1), coef_ref[dest])
        return piece_ref.at[i]

    exchange_kernel(count, make_piece, out_ref, *sems)


def exchange_sems(count):
    return [
        pltpu.SemaphoreType.DMA((count - 1,)),
        pltpu.SemaphoreType.DMA((count,)),
        pltpu.SemaphoreType.DMA,
    ]


def turn_and_return(pairing, x, coef):
    count = x.shape[0]
    return pl.pallas_call(
        partial(return_kernel, count),
        out_shape=jax.ShapeDtypeStruct(x.shape, x.dtype),
        in_specs=[
            pl.BlockSpec(memory_space=pltpu.SMEM),
            pl.BlockSpec(memory_space=pltpu.VMEM),
            pl.BlockSpec(memory_space=pltpu.VMEM),
        ],
        out_specs=pl.BlockSpec(memory_space=pl.ANY),
        scratch_shapes=[pltpu.VMEM(x.shape, x.dtype), *exchange_sems(count)],
        compiler_params=pltpu.CompilerParams(collective_id=2, has_side_effects=True),
    )(pairing, x, coef)


def exchange(x, collective_id):
    count = x.shape[0]
    return pl.pallas_call(
        partial(gather_kernel, count),
        out_shape=jax.ShapeDtypeStruct(x.shape, x.dtype),
        in_specs=[pl.BlockSpec(memory_space=pl.ANY)],
        out_specs=pl.BlockSpec(memory_space=pl.ANY),
        scratch_shapes=exchange_sems(count),
        compiler_params=pltpu.CompilerParams(
            collective_id=collective_id, has_side_effects=True
        ),
    )(x)


def quad_blocks(pairing, count, g):
    m0 = pairing[0, 0]
    m1 = pairing[1, 0]
    lower_mask = jnp.minimum(m0, m1)
    low_bits = jnp.int32(0)
    for bit in range(1, count.bit_length() - 1):
        low_bits = jnp.where(lower_mask >= (1 << bit), (1 << bit) - 1, low_bits)
    rest = g & low_bits
    q0 = rest + 2 * (g - rest)
    return q0, q0 ^ m0, q0 ^ m1, q0 ^ (count - 1)


def lane_bit(shape, bit):
    return (lax.broadcasted_iota(jnp.int32, shape, 1) & (1 << bit)) != 0


def to_bands(block):
    w = block.shape[0]
    for bit in range(w.bit_length() - 1):
        block = jnp.where(
            lane_bit(block.shape, bit), pltpu.roll(block, w - (1 << bit), 0), block
        )
    return jnp.concatenate([block[w - BAND :], block[:BAND]], axis=0)


def from_bands(bands):
    w = bands.shape[1]
    block = jnp.concatenate(
        [bands[BAND:], jnp.zeros((w - 2 * BAND, w), jnp.float32), bands[:BAND]], axis=0
    )
    for bit in range(w.bit_length() - 1):
        block = jnp.where(lane_bit(block.shape, bit), pltpu.roll(block, 1 << bit, 0), block)
    return block


def gram_kernel(pairing, x_0, x_1, x_2, x_3, band_ref):
    g = pl.program_id(0)
    w = x_0.shape[2]
    lo, hi = slice(0, w), slice(w, 2 * w)
    a = jnp.concatenate([x_0[0], x_1[0]], axis=1)
    b = jnp.concatenate([x_2[0], x_3[0]], axis=1)
    aa, bb, ba = dot_t(a, a), dot_t(b, b), dot_t(b, a)
    blocks = [aa[lo, lo], aa[hi, lo], aa[hi, hi], bb[lo, lo], bb[hi, lo], bb[hi, hi]]
    blocks += [ba[lo, lo], ba[lo, hi], ba[hi, lo], ba[hi, hi]]

    @pl.when(g == 0)
    def _():
        band_ref[...] = jnp.zeros_like(band_ref)

    for i, block in enumerate(blocks):
        start = pl.multiple_of((g * PAIRS + i) * 2 * BAND, 2 * BAND)
        band_ref[pl.ds(start, 2 * BAND), :] = to_bands(block)


def gram(pairing, x, total):
    count = x.shape[0]

    def member(i):
        return pl.BlockSpec(
            (1, *x.shape[1:]), lambda g, pairing: (quad_blocks(pairing, count, g)[i], 0, 0)
        )

    return pl.pallas_call(
        gram_kernel,
        grid_spec=pltpu.PrefetchScalarGridSpec(
            num_scalar_prefetch=1,
            grid=(count // 4,),
            in_specs=[member(i) for i in range(4)],
            out_specs=pl.BlockSpec(memory_space=pltpu.VMEM),
        ),
        out_shape=jax.ShapeDtypeStruct((total, x.shape[2]), jnp.float32),
    )(pairing, x, x, x, x)


def sum_kernel(x_ref, out_ref, landed, part, slots, whole, send_sem, recv_sem):
    rows, cols = x_ref.shape[0], x_ref.shape[1]
    r, c = lax.axis_index("rows"), lax.axis_index("cols")
    barrier = pltpu.get_barrier_semaphore()
    for d in range(1, rows):
        pl.semaphore_signal(barrier, inc=1, device_id={"rows": (r + d) % rows}, device_id_type=MESH)
    for d in range(1, cols):
        pl.semaphore_signal(barrier, inc=1, device_id={"cols": (c + d) % cols}, device_id_type=MESH)
    pl.semaphore_wait(barrier, rows + cols - 2)

    def stage(number, axis, me, count, source, dest):
        copies = []
        for d in range(1, count):
            peer = (me + d) % count
            copy = pltpu.make_async_remote_copy(
                src_ref=source(peer),
                dst_ref=dest(d),
                send_sem=send_sem.at[number, d],
                recv_sem=recv_sem.at[number, d],
                device_id={axis: peer},
                device_id_type=MESH,
            )
            copy.start()
            copies.append(copy)
        for copy in copies:
            copy.wait_recv()
        return copies

    def finish(copies):
        for copy in copies:
            copy.wait_send()

    sent = stage(0, "rows", r, rows, lambda p: x_ref.at[p], lambda d: landed.at[d])
    total = x_ref[r]
    for d in range(1, rows):
        total = total + landed[d]
    part[...] = total
    sent += stage(1, "cols", c, cols, lambda p: part.at[p], lambda d: slots.at[d])
    total = part[c]
    for d in range(1, cols):
        total = total + slots[d]
    whole[c] = total
    sent += stage(2, "cols", c, cols, lambda p: whole.at[c], lambda d: whole.at[c])
    out_ref[r] = whole[...]
    sent += stage(3, "rows", r, rows, lambda p: whole, lambda d: out_ref.at[r])
    finish(sent)


def sum_all(x, rows, cols):
    total, width = x.shape
    piece = total // (rows * cols)
    peers = max(rows, cols)
    summed = pl.pallas_call(
        sum_kernel,
        out_shape=jax.ShapeDtypeStruct((rows, cols, piece, width), jnp.float32),
        in_specs=[pl.BlockSpec(memory_space=pltpu.VMEM)],
        out_specs=pl.BlockSpec(memory_space=pltpu.VMEM),
        scratch_shapes=[
            pltpu.VMEM((rows, cols, piece, width), jnp.float32),
            pltpu.VMEM((cols, piece, width), jnp.float32),
            pltpu.VMEM((cols, piece, width), jnp.float32),
            pltpu.VMEM((cols, piece, width), jnp.float32),
            pltpu.SemaphoreType.DMA((4, peers)),
            pltpu.SemaphoreType.DMA((4, peers)),
        ],
        compiler_params=pltpu.CompilerParams(collective_id=3, has_side_effects=True),
    )(x.reshape(rows, cols, piece, width))
    return summed.reshape(total, width)


def turn_pairs(gram, turn, pairs):
    _, depth, sides, w = gram.shape

    def lane(value):
        return pltpu.roll(value.reshape(depth * sides, w), w - 1, 1).reshape(depth, sides, w)

    def later(value):
        return jnp.concatenate([value[-1:], value[:-1]], axis=0)

    def sooner(value):
        return jnp.concatenate([value[1:], value[:1]], axis=0)

    def swap(value):
        return jnp.concatenate([value[:, pairs:], value[:, :pairs]], axis=1)

    def ahead(value):
        return jnp.stack([pltpu.roll(value, (BAND - r) % w, 1) if r != BAND else value for r in range(depth)])

    lower = lax.broadcasted_iota(jnp.int32, (depth, sides, w), 1) >= pairs

    @pl.loop(0, SHIFTS)
    def _(step):
        g_l, g_r = gram[0], gram[1]
        a, e, g = gram[0, BAND, :pairs], gram[1, BAND, pairs:], gram[1, BAND, :pairs]
        gap = e - a
        sign = jnp.where(gap >= 0.0, 1.0, -1.0)
        denom = jnp.abs(gap) + jnp.sqrt(gap * gap + 4.0 * g * g) + TIE_GUARD * (a + e)
        tangent = 2.0 * g * sign / denom
        cosine = 1.0 / jnp.sqrt(1.0 + tangent * tangent)
        sine = cosine * tangent
        c_2 = jnp.concatenate([cosine, cosine], axis=0)
        s_2 = jnp.concatenate([sine, sine], axis=0)
        c_d = ahead(c_2)
        s_d = ahead(jnp.concatenate([-sine, sine], axis=0))
        t_l = g_l * c_2 - g_r * s_2
        t_r = g_l * s_2 + g_r * c_2
        t_l = c_d * t_l + s_d * swap(t_l)
        t_r = lane(c_d * t_r + s_d * swap(t_r))
        gram[0] = jnp.where(lower, sooner(t_l), t_l)
        gram[1] = jnp.where(lower, t_r, later(t_r))
        v_l, v_r = turn[0], turn[1]
        turn[0] = v_l * c_2 - v_r * s_2
        turn[1] = later(lane(v_l * s_2 + v_r * c_2))


def rotate_kernel(groups, pairing, band_ref, coef_ref, turn_ref, gram, turn):
    w = band_ref.shape[1]
    pairs = 2 * groups
    lo, hi = slice(0, w), slice(w, 2 * w)

    def bands(g, i):
        start = (g * PAIRS + i) * 2 * BAND
        return band_ref[start : start + 2 * BAND, :]

    def reset_turns():
        shape = turn.shape
        one = lax.broadcasted_iota(jnp.int32, shape, 1) == BAND
        lower = lax.broadcasted_iota(jnp.int32, shape, 2) >= pairs
        right = lax.broadcasted_iota(jnp.int32, shape, 0) == 1
        turn[...] = jnp.where(one & (lower == right), 1.0, 0.0)

    def put_turns(slot):
        for g in range(groups):
            for p in range(2):
                at = 2 * g + p
                for row, side in ((lo, at), (hi, pairs + at)):
                    turn_ref[g, slot + p, row, lo] = from_bands(turn[0, :, side, :])
                    moved = from_bands(turn[1, :, side, :])
                    turn_ref[g, slot + p, row, hi] = pltpu.roll(moved, SHIFTS, 1)

    def put_gram(at, ll, lr, rl, rr):
        gram[0, :, at, :] = ll
        gram[1, :, at, :] = lr
        gram[0, :, pairs + at, :] = rl
        gram[1, :, pairs + at, :] = rr

    for g in range(groups):
        for p in range(2):
            below = bands(g, 3 * p + 1)
            above = to_bands(from_bands(below).T)
            put_gram(2 * g + p, bands(g, 3 * p), above, below, bands(g, 3 * p + 2))
    reset_turns()
    turn_pairs(gram, turn, pairs)
    put_turns(0)

    for g in range(groups):
        blocks = [from_bands(bands(g, 6 + i)) for i in range(4)]
        cross = jnp.concatenate(
            [
                jnp.concatenate([blocks[0], blocks[1]], axis=1),
                jnp.concatenate([blocks[2], blocks[3]], axis=1),
            ],
            axis=0,
        )
        half = dot(cross, turn_ref[g, 0])
        below = [
            dot_t(turn_ref[g, 1, :, lo], half[:, lo]),
            dot_t(turn_ref[g, 1, :, hi], half[:, hi]),
        ]
        a, b = 2 * g, 2 * g + 1
        a_lo, b_lo = gram[0, :, a, :], gram[0, :, b, :]
        a_hi = pltpu.roll(gram[1, :, pairs + a, :], SHIFTS, 1)
        b_hi = pltpu.roll(gram[1, :, pairs + b, :], SHIFTS, 1)
        put_gram(a, a_lo, to_bands(below[0].T), to_bands(below[0]), b_lo)
        put_gram(b, a_hi, to_bands(below[1].T), to_bands(below[1]), b_hi)
    reset_turns()
    turn_pairs(gram, turn, pairs)
    put_turns(2)

    for g in range(groups):
        q = quad_blocks(pairing, 4 * groups, g)
        for side, part in ((0, lo), (1, hi)):
            last = turn_ref.at[g, 2 + side]
            top = dot(turn_ref[g, 0, :, part], last[lo, :])
            bottom = dot(turn_ref[g, 1, :, part], last[hi, :])
            rows = [top[lo], top[hi], bottom[lo], bottom[hi]]
            for member, cols in ((side, lo), (2 + side, hi)):
                for i in range(4):
                    coef_ref[q[member], i * w : (i + 1) * w, :] = rows[member ^ i][:, cols]


def rotate(pairing, bands, groups):
    w = bands.shape[1]
    state = pltpu.VMEM((2, 2 * BAND, 4 * groups, w), jnp.float32)
    return pl.pallas_call(
        partial(rotate_kernel, groups),
        in_specs=[
            pl.BlockSpec(memory_space=pltpu.SMEM),
            pl.BlockSpec(memory_space=pltpu.VMEM),
        ],
        out_specs=pl.BlockSpec(memory_space=pltpu.VMEM),
        out_shape=jax.ShapeDtypeStruct((4 * groups, 4 * w, w), jnp.float32),
        scratch_shapes=[
            pltpu.VMEM((groups, 4, 2 * w, 2 * w), jnp.float32),
            state,
            state,
        ],
    )(pairing, bands)


def on_device(anomalies, pairing):
    count = lax.axis_size("cols")
    rows, width = anomalies.shape
    x = exchange(anomalies.reshape(count, rows // count, width), 1)
    split = lax.axis_size("rows")
    groups = count // 4
    unit = 8 * split * count
    total = -(-groups * PAIRS * 2 * BAND // unit) * unit
    bands = sum_all(gram(pairing, x, total), split, count)
    coef = rotate(pairing, bands, groups)
    return turn_and_return(pairing, x, coef).reshape(rows, width)


def solution(mesh):
    placed = (P("rows", "cols"), P())
    return jax.shard_map(
        on_device, mesh=mesh, in_specs=placed, out_specs=P("rows", "cols"), check_vma=False
    )
```
